32 devices in a mesh: dom: 8 (over z, x), band: 4 (over y, core).
Axes of the slice: x: 2, y: 2, z: 4, core: 2. Of those that a mesh axis runs over, the one named last changes fastest.
Arguments:
- orbitals: float32 [32, 96, 64, 128], P('band', 'dom'), may hold values from -1400 to 1400
- potential: float32 [96, 64, 128], P('dom'), may hold values from 0.1 to 2
Outputs:
- ortho_orbitals: float32 [32, 96, 64, 128], P('band', 'dom')
The draws below stay inside these ranges and needn't reach their ends.
All inputs are finite; a program needn't handle non-finite values.
Results may differ from the reference program's by a relative error of at most 0.0003.
Values sent between devices are 32-bit elements; how exact they have to be, the bound alone decides.
A program may use at most 64 MiB of HBM per device.

```python
import math
import jax
import jax.numpy as jnp
from jax import lax

NB = 32
NY = 64
NZ = 128
NX = 96


def draw_orbitals(key, part):
    key_base = jax.random.fold_in(key, 11)
    key_mix = jax.random.fold_in(key, 12)
    key_scale = jax.random.fold_in(key, 13)
    base = jnp.clip(jax.random.normal(key_base, (NB, NX, NY, NZ), jnp.float32), -6.0, 6.0)
    mixing = jnp.eye(NB, dtype=jnp.float32) + 0.7 * jnp.clip(jax.random.normal(key_mix, (NB, NB), jnp.float32), -3.0, 3.0) / math.sqrt(NB)
    scales = jnp.exp(jax.random.uniform(key_scale, (NB,), jnp.float32, 0.0, math.log(10.0)))
    mixed = jnp.einsum('ab,bxyz->axyz', mixing * scales[:, None], base, precision=lax.Precision.HIGHEST)
    rising = jnp.exp(0.6 * jnp.arange(NX, dtype=jnp.float32) / NX)
    return mixed * rising[None, :, None, None]


def shard_levels(own_key, shape, cuts, smallest, top_value):
    level = 1.0
    for position, shards_of in cuts:
        heights = jax.random.uniform(jax.random.fold_in(jax.random.fold_in(own_key, 6), position), (shards_of,), jnp.float32, smallest / len(cuts), top_value / len(cuts))
        level = level * jnp.repeat(jnp.exp(heights), shape[position] // shards_of).reshape((-1,) + (1,) * (len(shape) - 1 - position))
    return level


def setup_inputs(seed: int = 0) -> dict:
    keys = jax.random.split(jax.random.key(seed), 3)
    orbitals = draw_orbitals(jax.random.fold_in(keys[2], 71), 0)
    potential = jnp.clip(jnp.exp(math.log(2.0) - 2.9957323 * jax.random.uniform(keys[1], (NX, NY, NZ), jnp.float32) ** shard_levels(keys[1], (NX, NY, NZ), ((0, 8),), -0.2, 0.2)), 0.1, 2.0)
    return dict(orbitals=orbitals, potential=potential)


stencil_weights = [-5369.0 / 1800.0, 12.0 / 7.0, -15.0 / 56.0, 10.0 / 189.0, -1.0 / 112.0, 2.0 / 1925.0, -1.0 / 16632.0]
center_shift = 9.5
half_width = 7.5

def apply_hamiltonian(padded, field_potential):
    length = field_potential.shape[0]
    inner = padded[:, 6:6 + length]
    rows_y = inner.shape[2]
    rows_z = inner.shape[3]
    spread = jnp.pad(inner, ((0, 0), (0, 0), (6, 6), (6, 6)))
    laplace = 3.0 * stencil_weights[0] * inner
    for offset in range(1, 7):
        near = padded[:, 6 + offset:6 + offset + length] + padded[:, 6 - offset:6 - offset + length]
        near = near + spread[:, :, 6 + offset:6 + offset + rows_y, 6:6 + rows_z] + spread[:, :, 6 - offset:6 - offset + rows_y, 6:6 + rows_z]
        near = near + spread[:, :, 6:6 + rows_y, 6 + offset:6 + offset + rows_z] + spread[:, :, 6:6 + rows_y, 6 - offset:6 - offset + rows_z]
        laplace = laplace + stencil_weights[offset] * near
    return -0.5 * laplace + field_potential * inner

def reference(orbitals, potential):

    def filter_one(single):
        block = single[None]
        padded = jnp.pad(block, ((0, 0), (6, 6), (0, 0), (0, 0)))
        first = (apply_hamiltonian(padded, potential) - center_shift * block) / half_width
        padded_first = jnp.pad(first, ((0, 0), (6, 6), (0, 0), (0, 0)))
        second = 2.0 * (apply_hamiltonian(padded_first, potential) - center_shift * first) / half_width - block
        return second[0]
    filtered = lax.map(filter_one, orbitals)
    flat = filtered.reshape(NB, -1)
    correlation = jnp.dot(flat.astype(jnp.float32), flat.T.astype(jnp.float32), precision=lax.Precision.HIGHEST, preferred_element_type=jnp.float32)
    correlation = correlation / jnp.float32(NX * NY * NZ)
    lower = jnp.linalg.cholesky(correlation)
    inverse = lax.linalg.triangular_solve(lower, jnp.eye(NB, dtype=correlation.dtype), left_side=True, lower=True)
    result = jnp.dot(inverse.astype(jnp.float32), flat.astype(jnp.float32), precision=lax.Precision.HIGHEST, preferred_element_type=jnp.float32)
    return result.reshape(orbitals.shape)
```

```python
import functools
import jax
import jax.numpy as jnp
from jax import lax
from jax.experimental import pallas as pl
from jax.experimental.pallas import tpu as pltpu
from jax.sharding import PartitionSpec as P

stencil_weights = [
    -5369.0 / 1800.0,
    12.0 / 7.0,
    -15.0 / 56.0,
    10.0 / 189.0,
    -1.0 / 112.0,
    2.0 / 1925.0,
    -1.0 / 16632.0,
]
center_shift = 9.5
half_width = 7.5
reach = 6
pad = 8
scaled = [-0.5 * w / half_width for w in stencil_weights]
HIGHEST = lax.Precision.HIGHEST
MESH = pl.DeviceIdType.MESH


def divisor(n, options):
    for c in options:
        if n % c == 0:
            return c
    return 1


def packed_rows(total, nz):
    fold = nz // total if total < nz and nz % total == 0 else 1
    return total // fold if total % (8 * fold) == 0 else total


def kernel(
    doms, bands, nb, nx, ny, nz,
    orb, pot, out,
    bz, u, f, own_f, ret_f, potb, cells, obuf, gs, ar1, ar2, inv,
    own_sem, pot_sem, pot_s, pot_r, swap_s, swap_r, h1_s, h1_r, h2_s, h2_r,
    ret_s, ret_r, core_s, core_r, loc_s, y_s, y_r,
    r1_s, r1_r, r2_s, r2_r, out_s, out_r, out_l,
):
    half = nb // 2
    planes = 2 * nx
    total = nb * bands
    group = 2 * bands
    chips = bands // 2
    slab = nx * ny
    part = slab // 2
    share = part // chips
    dom = lax.axis_index("dom")
    band = lax.axis_index("band")
    layer = dom // 2
    layers = doms // 2
    side = dom % 2
    row = band // 2
    core = band % 2
    base = layer * 2
    me = side * bands + band
    partner = {"dom": base + 1 - side, "band": band}
    sibling = {"dom": dom, "band": row * 2 + 1 - core}
    inner, outer = 1 - side, side

    def peer_id(j):
        g = (me + j) % group
        return {"dom": base + g // bands, "band": g % bands}

    def layer_id(j):
        return {"dom": ((layer + j) % layers) * 2 + side, "band": band}

    barrier = pltpu.get_barrier_semaphore()
    for j in range(1, group):
        pl.semaphore_signal(barrier, inc=1, device_id=peer_id(j), device_id_type=MESH)
    for j in range(1, layers):
        pl.semaphore_signal(barrier, inc=1, device_id=layer_id(j), device_id_type=MESH)
    pl.semaphore_wait(barrier, group - 1 + layers - 1)

    def remote(src, dst, s, r, dev):
        return pltpu.make_async_remote_copy(
            src_ref=src, dst_ref=dst, send_sem=s, recv_sem=r, device_id=dev, device_id_type=MESH
        )

    rows = pl.ds(pad, ny)

    def swap(o, p):
        first = (outer if p == 0 else inner) * reach
        return remote(
            orb.at[(1 - side) * half + o, pl.ds(first, reach)],
            u.at[o, pl.ds(reach + side * nx + first, reach), rows],
            swap_s.at[p, o], swap_r.at[p, o], partner,
        )

    pot_share = slab // bands
    pot_rows = pl.ds(pl.multiple_of(band * pot_share, 8), pot_share)
    my_pot = pl.ds(pl.multiple_of(side * slab + band * pot_share, 8), pot_share)
    got_pot = pl.ds(pl.multiple_of((1 - side) * slab + band * pot_share, 8), pot_share)
    swap_pot = remote(pot.at[pot_rows], potb.at[my_pot], pot_s.at[0], pot_r.at[0], partner)

    def pass_pot(j):
        return remote(
            potb.at[got_pot], potb.at[got_pot], pot_s.at[j], pot_r.at[j],
            {"dom": dom, "band": (band + j) % bands},
        )

    def own(o):
        return pltpu.make_async_copy(
            orb.at[side * half + o], u.at[o, pl.ds(reach + side * nx, nx), rows], own_sem.at[o]
        )

    own_pot = pltpu.make_async_copy(
        pot, potb.at[pl.ds(pl.multiple_of(side * slab, 8), slab)], pot_sem
    )

    swap_pot.start()
    for o in range(half):
        for p in range(2):
            swap(o, p).start()
    for o in range(half):
        own(o).start()
    own_pot.start()

    def up(buf, o, s, r):
        return remote(
            buf.at[o, pl.ds(planes, reach), rows], buf.at[o, pl.ds(0, reach), rows],
            s.at[0, o], r.at[0, o], {"dom": dom + 2, "band": band},
        )

    def down(buf, o, s, r):
        return remote(
            buf.at[o, pl.ds(reach, reach), rows], buf.at[o, pl.ds(planes + reach, reach), rows],
            s.at[1, o], r.at[1, o], {"dom": dom - 2, "band": band},
        )

    has_up = layer < layers - 1
    has_down = layer > 0

    def send_face(buf, o, s, r, which):
        @pl.when(jnp.logical_and(has_up, side == which))
        def _():
            up(buf, o, s, r).start()

        @pl.when(jnp.logical_and(has_down, side == 1 - which))
        def _():
            down(buf, o, s, r).start()

    def wait_halos(buf, o, s, r):
        @pl.when(has_down)
        def _():
            up(buf, o, s, r).wait_recv()

        @pl.when(has_up)
        def _():
            down(buf, o, s, r).wait_recv()

    distance = jnp.abs(
        lax.broadcasted_iota(jnp.int32, (nz, nz), 0) - lax.broadcasted_iota(jnp.int32, (nz, nz), 1)
    )
    banded = jnp.zeros((nz, nz), jnp.float32)
    for k in range(1, reach + 1):
        banded = jnp.where(distance == k, jnp.float32(scaled[k]), banded)
    bz[...] = banded
    edge = jnp.zeros((planes + 2 * reach, pad, nz), jnp.float32)
    for buf in (u, f):
        for o in range(half):
            buf[o, :, pl.ds(0, pad), :] = edge
            buf[o, :, pl.ds(pad + ny, pad), :] = edge
    empty = jnp.zeros((reach, ny, nz), jnp.float32)
    for buf in (u, f):
        for o in range(half):
            @pl.when(jnp.logical_not(has_down))
            def _():
                buf[o, pl.ds(0, reach), rows, :] = empty

            @pl.when(jnp.logical_not(has_up))
            def _():
                buf[o, pl.ds(planes + reach, reach), rows, :] = empty

    for q in range(1, chips):
        @pl.when(row < q)
        def _():
            for i in range(q * 2 * nb, (q + 1) * 2 * nb):
                for p in range(1, chips):
                    first = pl.multiple_of(i * part + ((row + p) % chips) * share, 8)
                    cells[pl.ds(first, share), :] = jnp.zeros((share, nz), jnp.float32)

    def apply(buf, o, first, count, emit):
        step = divisor(count, (4, 3, 2))

        def body(t, carry):
            x0 = first + t * step
            centre = [buf[o, reach + x0 + i, pl.ds(pad, ny), :] for i in range(step)]
            along_z = jnp.dot(
                jnp.concatenate(centre, axis=0), bz[...], precision=HIGHEST,
                preferred_element_type=jnp.float32,
            )
            for i in range(step):
                x = reach + x0 + i
                weight = potb[pl.ds(pl.multiple_of((x0 + i) * ny, 8), ny), :] * (1.0 / half_width) + (
                    3.0 * scaled[0] - center_shift / half_width
                )
                acc = along_z[i * ny:(i + 1) * ny] + weight * centre[i]
                for k in range(1, reach + 1):
                    near = buf[o, x + k, pl.ds(pad, ny), :] + buf[o, x - k, pl.ds(pad, ny), :]
                    near = near + (
                        buf[o, x, pl.ds(pad + k, ny), :] + buf[o, x, pl.ds(pad - k, ny), :]
                    )
                    acc = acc + scaled[k] * near
                emit(x0 + i, acc)
            return carry

        lax.fori_loop(0, count // step, body, 0)

    def first_term(o, first, count):
        def emit(x, acc):
            f[o, reach + x, pl.ds(pad, ny), :] = acc

        apply(u, o, first, count, emit)

    def second_term(o, slab_side, which, dst, k):
        def emit(x, acc):
            start = pl.multiple_of((x - slab_side * nx) * ny, 8)
            dst[k, pl.ds(start, ny), :] = 2.0 * acc - u[o, reach + x, pl.ds(pad, ny), :]

        apply(f, o, slab_side * nx + which * reach, reach, emit)

    def y_copy(j, k, h, p):
        to = (row + j) % chips
        at = ((to + p) % chips) * share
        return remote(
            own_f.at[k, pl.ds(pl.multiple_of(h * part + at, 8), share)],
            cells.at[pl.ds(pl.multiple_of((band * nb + k) * part + at, 8), share)],
            y_s.at[j - 1, h, k, p], y_r.at[j - 1, core, k, p],
            {"dom": dom, "band": to * 2 + h},
        )

    def y_got(j, c, k, p):
        to = row
        at = ((to + p) % chips) * share
        from_band = ((row - j + chips) % chips) * 2 + c
        return remote(
            own_f.at[k, pl.ds(pl.multiple_of(at, 8), share)],
            cells.at[pl.ds(pl.multiple_of((from_band * nb + k) * part + at, 8), share)],
            y_s.at[j - 1, 0, k, p], y_r.at[j - 1, c, k, p],
            {"dom": dom, "band": ((row + j) % chips) * 2},
        )

    def core_copy(k):
        return remote(
            own_f.at[k, pl.ds(pl.multiple_of((1 - core) * part, 8), part)],
            cells.at[pl.ds(pl.multiple_of((band * nb + k) * part, 8), part)],
            core_s.at[k], core_r.at[k], sibling,
        )

    def local_copy(k):
        return pltpu.make_async_copy(
            own_f.at[k, pl.ds(pl.multiple_of(core * part, 8), part)],
            cells.at[pl.ds(pl.multiple_of((band * nb + k) * part, 8), part)],
            loc_s.at[k],
        )

    def spread(k, h):
        for j in range(1, chips):
            y_copy(j, k, h, 0).start()

        @pl.when(h != core)
        def _():
            core_copy(k).start()

        @pl.when(h == core)
        def _():
            local_copy(k).start()

    def spread_rest(k, h):
        for j in range(1, chips):
            @pl.when((row + j) % chips > row)
            def _():
                for p in range(1, chips):
                    y_copy(j, k, h, p).start()

    def back(o, h):
        at = pl.ds(pl.multiple_of(h * part, 8), part)
        return remote(
            ret_f.at[o, at], own_f.at[side * half + o, at], ret_s.at[h, o], ret_r.at[h, o], partner
        )

    def came(o, h):
        at = pl.ds(pl.multiple_of(h * part, 8), part)
        return remote(
            ret_f.at[o, at], own_f.at[(1 - side) * half + o, at], ret_s.at[h, o], ret_r.at[h, o], partner
        )

    def finish(o, which):
        k = side * half + o
        second_term(o, side, which, own_f, k)
        spread(k, which)
        spread_rest(k, which)
        second_term(o, 1 - side, 1 - which, ret_f, o)
        back(o, 1 - which).start()

    def returned(o, which):
        came(o, which).wait_recv()
        spread((1 - side) * half + o, which)

    def late(o, which):
        spread_rest((1 - side) * half + o, which)

    swap_pot.wait_recv()
    for j in range(1, bands):
        pass_pot(j).start()
    for o in range(min(2, half)):
        own(o).wait()
        send_face(u, o, h1_s, h1_r, 1)
    own_pot.wait()

    for o in range(half):
        swap(o, 0).wait_recv()
        send_face(u, o, h1_s, h1_r, 0)
        if o == 0:
            for j in range(1, bands):
                pass_pot(j).wait_recv()
        swap(o, 1).wait_recv()
        first_term(o, reach, planes - 2 * reach)
        if o > 0:
            wait_halos(f, o - 1, h2_s, h2_r)
            finish(o - 1, outer)
        wait_halos(u, o, h1_s, h1_r)
        first_term(o, 0, reach)
        first_term(o, planes - reach, reach)
        send_face(f, o, h2_s, h2_r, 1)
        send_face(f, o, h2_s, h2_r, 0)
        if o + 2 < half:
            own(o + 2).wait()
            send_face(u, o + 2, h1_s, h1_r, 1)
        finish(o, inner)
    returned(0, inner)
    wait_halos(f, half - 1, h2_s, h2_r)
    finish(half - 1, outer)
    returned(0, outer)
    for o in range(1, half):
        returned(o, inner)
        late(o - 1, inner) if o < half - 1 else None
        returned(o, outer)
        late(o - 1, outer) if o < half - 1 else None
    for o in range(max(half - 2, 0), half):
        late(o, inner)
        late(o, outer)

    for k in range(nb):
        local_copy(k).wait()
        core_copy(k).wait_recv()
        for j in range(1, chips):
            for c in range(2):
                y_got(j, c, k, 0).wait_recv()

    packed = packed_rows(total, nz)
    chunk = divisor(share, (16, 8))

    def gather(first):
        return jnp.concatenate(
            [cells[pl.ds(first + i, total, stride=part), :] for i in range(chunk)], axis=1
        )

    mine = row * share

    def gram_body(t, acc):
        x = gather(mine + t * chunk)
        return acc + lax.dot_general(
            x, x, (((1,), (1,)), ((), ())), precision=HIGHEST, preferred_element_type=jnp.float32
        )

    gram = lax.fori_loop(0, share // chunk, gram_body, jnp.zeros((total, total), jnp.float32))
    gram = jnp.concatenate(
        [gram[i * packed:(i + 1) * packed] for i in range(total // packed)], axis=1
    )
    gs[0] = gram
    ar1[me] = gram

    def reduce_1(j):
        return remote(gs.at[0], ar1.at[me], r1_s.at[j - 1], r1_r.at[j - 1], peer_id(j))

    def reduce_2(j):
        return remote(gs.at[1], ar2.at[layer], r2_s.at[j - 1], r2_r.at[j - 1], layer_id(j))

    for j in range(1, group):
        reduce_1(j).start()
    for j in range(1, group):
        reduce_1(j).wait_recv()
    total_1 = ar1[0]
    for j in range(1, group):
        total_1 = total_1 + ar1[j]
    gs[1] = total_1
    ar2[layer] = total_1
    for j in range(1, layers):
        reduce_2(j).start()
    for j in range(1, layers):
        reduce_2(j).wait_recv()
    work = ar2[0]
    for j in range(1, layers):
        work = work + ar2[j]

    work = jnp.concatenate(
        [work[:, i * total:(i + 1) * total] for i in range(total // packed)], axis=0
    )
    work = jnp.concatenate([work, jnp.zeros((total, total), jnp.float32)], axis=1)
    lane = lax.broadcasted_iota(jnp.int32, work.shape, 1)
    line = lax.broadcasted_iota(jnp.int32, work.shape, 0)
    work = work / jnp.float32(slab * doms * nz)
    work = jnp.where(lane == line + total, jnp.float32(1.0), work)
    for k in range(total):
        root = jnp.sqrt(work[k:k + 1, k:k + 1])
        scale = 1.0 / root
        pivot = work[k:k + 1, :] * scale
        column = work[:, k:k + 1] * scale
        work = jnp.where(line > k, work - column * pivot, jnp.where(line == k, pivot, work))
    pair = 2 * nb
    for q in range(chips):
        inv[q] = work[q * pair:(q + 1) * pair, total:2 * total]

    pieces = divisor(share // chunk, (4, 3, 2))
    piece = share // pieces
    obuf3 = obuf.reshape(pair, part, nz)

    def give(p, s):
        at = pl.multiple_of(((row + p) % chips) * share + s * piece, 8)
        return remote(
            obuf3.at[pl.ds((1 - core) * nb, nb), pl.ds(at, piece)],
            out.at[:, pl.ds(core * part + at, piece)],
            out_s.at[p, s], out_r.at[p, s], sibling,
        )

    def keep(p, s):
        at = pl.multiple_of(((row + p) % chips) * share + s * piece, 8)
        return pltpu.make_async_copy(
            obuf3.at[pl.ds(core * nb, nb), pl.ds(at, piece)],
            out.at[:, pl.ds(core * part + at, piece)], out_l.at[p, s],
        )

    for p in range(chips):
        if p > 0:
            for j in range(1, chips):
                @pl.when((row - j + chips) % chips < row)
                def _():
                    for k in range(nb):
                        for c in range(2):
                            y_got(j, c, k, p).wait_recv()
        at_part = ((row + p) % chips) * share

        def piece_body(s, carry):
            def ortho_body(t, carry):
                first = at_part + s * piece + t * chunk
                y = jnp.dot(inv[row], gather(first), precision=HIGHEST, preferred_element_type=jnp.float32)
                for i in range(chunk):
                    obuf[pl.ds(first + i, pair, stride=part), :] = y[:, i * nz:(i + 1) * nz]
                return carry

            lax.fori_loop(0, piece // chunk, ortho_body, 0)
            give(p, s).start()
            keep(p, s).start()
            return carry

        lax.fori_loop(0, pieces, piece_body, 0)

    swap_pot.wait_send()
    for j in range(1, bands):
        pass_pot(j).wait_send()
    for o in range(half):
        for p in range(2):
            swap(o, p).wait_send()
            back(o, p).wait_send()

        @pl.when(has_up)
        def _():
            up(u, o, h1_s, h1_r).wait_send()
            up(f, o, h2_s, h2_r).wait_send()

        @pl.when(has_down)
        def _():
            down(u, o, h1_s, h1_r).wait_send()
            down(f, o, h2_s, h2_r).wait_send()

    for k in range(nb):
        core_copy(k).wait_send()
        for j in range(1, chips):
            for h in range(2):
                y_copy(j, k, h, 0).wait_send()

            @pl.when((row + j) % chips > row)
            def _():
                for h in range(2):
                    for p in range(1, chips):
                        y_copy(j, k, h, p).wait_send()
    for j in range(1, group):
        reduce_1(j).wait_send()
    for j in range(1, layers):
        reduce_2(j).wait_send()
    for p in range(chips):
        for s in range(pieces):
            keep(p, s).wait()
            give(p, s).wait()


def deliver(held, out, sem):
    copy = pltpu.make_async_copy(held, out, sem)
    copy.start()
    copy.wait()


def shards(doms, bands, orbitals, potential):
    nb, nx, ny, nz = orbitals.shape
    half = nb // 2
    total = nb * bands
    group = 2 * bands
    layers = doms // 2
    chips = bands // 2
    slab = nx * ny
    part = slab // 2
    share = part // chips
    pair = 2 * nb
    dma = pltpu.SemaphoreType.DMA
    f32 = jnp.float32
    packed = packed_rows(total, nz)
    wide = total * total // packed
    pieces = divisor(share // divisor(share, (16, 8)), (4, 3, 2))
    others = max(chips - 1, 1)
    out = pl.pallas_call(
        functools.partial(kernel, doms, bands, nb, nx, ny, nz),
        out_shape=pltpu.VMEM((nb, slab, nz), f32),
        in_specs=[
            pl.BlockSpec(memory_space=pl.ANY),
            pl.BlockSpec(memory_space=pl.ANY),
        ],
        out_specs=pl.BlockSpec(memory_space=pltpu.VMEM),
        scratch_shapes=[
            pltpu.VMEM((nz, nz), f32),
            pltpu.VMEM((half, 2 * nx + 2 * reach, ny + 2 * pad, nz), f32),
            pltpu.VMEM((half, 2 * nx + 2 * reach, ny + 2 * pad, nz), f32),
            pltpu.VMEM((nb, slab, nz), f32),
            pltpu.VMEM((half, slab, nz), f32),
            pltpu.VMEM((2 * slab, nz), f32),
            pltpu.VMEM((total * part, nz), f32),
            pltpu.VMEM((pair * part, nz), f32),
            pltpu.VMEM((2, packed, wide), f32),
            pltpu.VMEM((group, packed, wide), f32),
            pltpu.VMEM((layers, packed, wide), f32),
            pltpu.VMEM((chips, pair, total), f32),
            dma((half,)),
            dma,
            dma((bands,)),
            dma((bands,)),
            dma((2, half)),
            dma((2, half)),
            dma((2, half)),
            dma((2, half)),
            dma((2, half)),
            dma((2, half)),
            dma((2, half)),
            dma((2, half)),
            dma((nb,)),
            dma((nb,)),
            dma((nb,)),
            dma((others, 2, nb, chips)),
            dma((others, 2, nb, chips)),
            dma((group - 1,)),
            dma((group - 1,)),
            dma((max(layers - 1, 1),)),
            dma((max(layers - 1, 1),)),
            dma((chips, pieces)),
            dma((chips, pieces)),
            dma((chips, pieces)),
        ],
        compiler_params=pltpu.CompilerParams(
            collective_id=0, has_side_effects=True, vmem_limit_bytes=60 * 1024 * 1024
        ),
    )(orbitals, potential.reshape(slab, nz))
    out = pl.pallas_call(
        deliver,
        out_shape=jax.ShapeDtypeStruct((nb, slab, nz), f32),
        in_specs=[pl.BlockSpec(memory_space=pl.ANY)],
        out_specs=pl.BlockSpec(memory_space=pl.ANY),
        scratch_shapes=[dma],
        compiler_params=pltpu.CompilerParams(vmem_limit_bytes=16 * 1024 * 1024),
    )(pltpu.with_memory_space_constraint(out, pltpu.VMEM))
    return out.reshape(orbitals.shape)


def solution(mesh):
    in_specs = (P("band", "dom", None, None), P("dom", None, None))
    out_specs = P("band", "dom", None, None)
    body = functools.partial(shards, mesh.shape["dom"], mesh.shape["band"])
    return jax.shard_map(body, mesh=mesh, in_specs=in_specs, out_specs=out_specs, check_vma=False)
```

```python
import functools
import jax
import jax.numpy as jnp
from jax import lax
from jax.experimental import pallas as pl
from jax.experimental.pallas import tpu as pltpu
from jax.sharding import PartitionSpec as P

stencil_weights = [
    -5369.0 / 1800.0,
    12.0 / 7.0,
    -15.0 / 56.0,
    10.0 / 189.0,
    -1.0 / 112.0,
    2.0 / 1925.0,
    -1.0 / 16632.0,
]
center_shift = 9.5
half_width = 7.5
reach = 6
pad = 8
scaled = [-0.5 * w / half_width for w in stencil_weights]
HIGHEST = lax.Precision.HIGHEST
HIGH = lax.Precision.HIGH
MESH = pl.DeviceIdType.MESH


def divisor(n, options):
    for c in options:
        if n % c == 0:
            return c
    return 1


def packed_rows(total, nz):
    fold = nz // total if total < nz and nz % total == 0 else 1
    return total // fold if total % (8 * fold) == 0 else total


def kernel(
    doms, bands, nb, nx, ny, nz,
    orb, pot, out,
    bz, u, f, own_f, ret_f, potb, cells, obuf, gs, ar1, ar2, inv,
    own_sem, pot_sem, pot_s, pot_r, swap_s, swap_r, h1_s, h1_r, h2_s, h2_r,
    ret_s, ret_r, core_s, core_r, loc_s, y_s, y_r,
    r1_s, r1_r, r2_s, r2_r, out_s, out_r, out_l,
):
    half = nb // 2
    planes = 2 * nx
    total = nb * bands
    group = 2 * bands
    chips = bands // 2
    slab = nx * ny
    part = slab // 2
    share = part // chips
    dom = lax.axis_index("dom")
    band = lax.axis_index("band")
    layer = dom // 2
    layers = doms // 2
    side = dom % 2
    row = band // 2
    core = band % 2
    base = layer * 2
    me = side * bands + band
    partner = {"dom": base + 1 - side, "band": band}
    sibling = {"dom": dom, "band": row * 2 + 1 - core}
    inner, outer = 1 - side, side

    def peer_id(j):
        g = (me + j) % group
        return {"dom": base + g // bands, "band": g % bands}

    def layer_id(j):
        return {"dom": ((layer + j) % layers) * 2 + side, "band": band}

    barrier = pltpu.get_barrier_semaphore()
    for j in range(1, group):
        pl.semaphore_signal(barrier, inc=1, device_id=peer_id(j), device_id_type=MESH)
    for j in range(1, layers):
        pl.semaphore_signal(barrier, inc=1, device_id=layer_id(j), device_id_type=MESH)
    pl.semaphore_wait(barrier, group - 1 + layers - 1)

    def remote(src, dst, s, r, dev):
        return pltpu.make_async_remote_copy(
            src_ref=src, dst_ref=dst, send_sem=s, recv_sem=r, device_id=dev, device_id_type=MESH
        )

    rows = pl.ds(pad, ny)

    def swap(o, p):
        first = (outer if p == 0 else inner) * reach
        return remote(
            orb.at[(1 - side) * half + o, pl.ds(first, reach)],
            u.at[o, pl.ds(reach + side * nx + first, reach), rows],
            swap_s.at[p, o], swap_r.at[p, o], partner,
        )

    pot_share = slab // bands
    pot_rows = pl.ds(pl.multiple_of(band * pot_share, 8), pot_share)
    my_pot = pl.ds(pl.multiple_of(side * slab + band * pot_share, 8), pot_share)
    got_pot = pl.ds(pl.multiple_of((1 - side) * slab + band * pot_share, 8), pot_share)
    swap_pot = remote(pot.at[pot_rows], potb.at[my_pot], pot_s.at[0], pot_r.at[0], partner)

    def pass_pot(j):
        return remote(
            potb.at[got_pot], potb.at[got_pot], pot_s.at[j], pot_r.at[j],
            {"dom": dom, "band": (band + j) % bands},
        )

    def own(o):
        return pltpu.make_async_copy(
            orb.at[side * half + o], u.at[o, pl.ds(reach + side * nx, nx), rows], own_sem.at[o]
        )

    own_pot = pltpu.make_async_copy(
        pot, potb.at[pl.ds(pl.multiple_of(side * slab, 8), slab)], pot_sem
    )

    swap_pot.start()
    for o in range(half):
        for p in range(2):
            swap(o, p).start()
    for o in range(half):
        own(o).start()
    own_pot.start()

    def up(buf, o, s, r):
        return remote(
            buf.at[o, pl.ds(planes, reach), rows], buf.at[o, pl.ds(0, reach), rows],
            s.at[0, o], r.at[0, o], {"dom": dom + 2, "band": band},
        )

    def down(buf, o, s, r):
        return remote(
            buf.at[o, pl.ds(reach, reach), rows], buf.at[o, pl.ds(planes + reach, reach), rows],
            s.at[1, o], r.at[1, o], {"dom": dom - 2, "band": band},
        )

    has_up = layer < layers - 1
    has_down = layer > 0

    def send_face(buf, o, s, r, which):
        @pl.when(jnp.logical_and(has_up, side == which))
        def _():
            up(buf, o, s, r).start()

        @pl.when(jnp.logical_and(has_down, side == 1 - which))
        def _():
            down(buf, o, s, r).start()

    def wait_halos(buf, o, s, r):
        @pl.when(has_down)
        def _():
            up(buf, o, s, r).wait_recv()

        @pl.when(has_up)
        def _():
            down(buf, o, s, r).wait_recv()

    distance = jnp.abs(
        lax.broadcasted_iota(jnp.int32, (nz, nz), 0) - lax.broadcasted_iota(jnp.int32, (nz, nz), 1)
    )
    banded = jnp.zeros((nz, nz), jnp.float32)
    for k in range(1, reach + 1):
        banded = jnp.where(distance == k, jnp.float32(scaled[k]), banded)
    bz[...] = banded
    edge = jnp.zeros((planes + 2 * reach, pad, nz), jnp.float32)
    for buf in (u, f):
        for o in range(half):
            buf[o, :, pl.ds(0, pad), :] = edge
            buf[o, :, pl.ds(pad + ny, pad), :] = edge
    empty = jnp.zeros((reach, ny, nz), jnp.float32)
    for buf in (u, f):
        for o in range(half):
            @pl.when(jnp.logical_not(has_down))
            def _():
                buf[o, pl.ds(0, reach), rows, :] = empty

            @pl.when(jnp.logical_not(has_up))
            def _():
                buf[o, pl.ds(planes + reach, reach), rows, :] = empty

    for q in range(1, chips):
        @pl.when(row < q)
        def _():
            for p in range(1, chips):
                at = ((row + p) % chips) * share
                cells[pl.ds(at, share), pl.ds(q * 2 * nb, 2 * nb), :] = jnp.zeros(
                    (share, 2 * nb, nz), jnp.float32
                )

    def apply(buf, o, first, count, emit):
        step = divisor(count, (4, 3, 2))

        def body(t, carry):
            x0 = first + t * step
            centre = [buf[o, reach + x0 + i, pl.ds(pad, ny), :] for i in range(step)]
            along_z = jnp.dot(
                jnp.concatenate(centre, axis=0), bz[...], precision=HIGHEST,
                preferred_element_type=jnp.float32,
            )
            for i in range(step):
                x = reach + x0 + i
                weight = potb[pl.ds(pl.multiple_of((x0 + i) * ny, 8), ny), :] * (1.0 / half_width) + (
                    3.0 * scaled[0] - center_shift / half_width
                )
                acc = along_z[i * ny:(i + 1) * ny] + weight * centre[i]
                for k in range(1, reach + 1):
                    near = buf[o, x + k, pl.ds(pad, ny), :] + buf[o, x - k, pl.ds(pad, ny), :]
                    near = near + (
                        buf[o, x, pl.ds(pad + k, ny), :] + buf[o, x, pl.ds(pad - k, ny), :]
                    )
                    acc = acc + scaled[k] * near
                emit(x0 + i, acc)
            return carry

        lax.fori_loop(0, count // step, body, 0)

    def first_term(o, first, count):
        def emit(x, acc):
            f[o, reach + x, pl.ds(pad, ny), :] = acc

        apply(u, o, first, count, emit)

    def second_term(o, slab_side, which, dst, k):
        def emit(x, acc):
            start = pl.multiple_of((x - slab_side * nx) * ny, 8)
            dst[k, pl.ds(start, ny), :] = 2.0 * acc - u[o, reach + x, pl.ds(pad, ny), :]

        apply(f, o, slab_side * nx + which * reach, reach, emit)

    def y_copy(j, k, h, p):
        to = (row + j) % chips
        at = ((to + p) % chips) * share
        return remote(
            own_f.at[k, pl.ds(pl.multiple_of(h * part + at, 8), share)],
            cells.at[pl.ds(at, share), band * nb + k],
            y_s.at[j - 1, h, k, p], y_r.at[j - 1, core, k, p],
            {"dom": dom, "band": to * 2 + h},
        )

    def y_got(j, c, k, p):
        to = row
        at = ((to + p) % chips) * share
        from_band = ((row - j + chips) % chips) * 2 + c
        return remote(
            own_f.at[k, pl.ds(pl.multiple_of(at, 8), share)],
            cells.at[pl.ds(at, share), from_band * nb + k],
            y_s.at[j - 1, 0, k, p], y_r.at[j - 1, c, k, p],
            {"dom": dom, "band": ((row + j) % chips) * 2},
        )

    def core_copy(k):
        return remote(
            own_f.at[k, pl.ds(pl.multiple_of((1 - core) * part, 8), part)],
            cells.at[:, band * nb + k],
            core_s.at[k], core_r.at[k], sibling,
        )

    def local_copy(k):
        return pltpu.make_async_copy(
            own_f.at[k, pl.ds(pl.multiple_of(core * part, 8), part)],
            cells.at[:, band * nb + k],
            loc_s.at[k],
        )

    def spread(k, h):
        for j in range(1, chips):
            y_copy(j, k, h, 0).start()

        @pl.when(h != core)
        def _():
            core_copy(k).start()

        @pl.when(h == core)
        def _():
            local_copy(k).start()

    def spread_rest(k, h):
        for j in range(1, chips):
            @pl.when((row + j) % chips > row)
            def _():
                for p in range(1, chips):
                    y_copy(j, k, h, p).start()

    def back(o, h):
        at = pl.ds(pl.multiple_of(h * part, 8), part)
        return remote(
            ret_f.at[o, at], own_f.at[side * half + o, at], ret_s.at[h, o], ret_r.at[h, o], partner
        )

    def came(o, h):
        at = pl.ds(pl.multiple_of(h * part, 8), part)
        return remote(
            ret_f.at[o, at], own_f.at[(1 - side) * half + o, at], ret_s.at[h, o], ret_r.at[h, o], partner
        )

    def finish(o, which):
        k = side * half + o
        second_term(o, side, which, own_f, k)
        spread(k, which)
        spread_rest(k, which)
        second_term(o, 1 - side, 1 - which, ret_f, o)
        back(o, 1 - which).start()

    def returned(o, which):
        came(o, which).wait_recv()
        spread((1 - side) * half + o, which)

    def late(o, which):
        spread_rest((1 - side) * half + o, which)

    swap_pot.wait_recv()
    for j in range(1, bands):
        pass_pot(j).start()
    for o in range(min(2, half)):
        own(o).wait()
        send_face(u, o, h1_s, h1_r, 1)
    own_pot.wait()

    for o in range(half):
        swap(o, 0).wait_recv()
        send_face(u, o, h1_s, h1_r, 0)
        if o == 0:
            for j in range(1, bands):
                pass_pot(j).wait_recv()
        swap(o, 1).wait_recv()
        first_term(o, reach, planes - 2 * reach)
        if o > 0:
            wait_halos(f, o - 1, h2_s, h2_r)
            finish(o - 1, outer)
        wait_halos(u, o, h1_s, h1_r)
        first_term(o, 0, reach)
        first_term(o, planes - reach, reach)
        send_face(f, o, h2_s, h2_r, 1)
        send_face(f, o, h2_s, h2_r, 0)
        if o + 2 < half:
            own(o + 2).wait()
            send_face(u, o + 2, h1_s, h1_r, 1)
        finish(o, inner)
    units = [(o, w) for o in range(half) for w in (inner, outer)]
    ahead = 4
    returned(*units[0])
    wait_halos(f, half - 1, h2_s, h2_r)
    finish(half - 1, outer)
    for i in range(1, len(units)):
        returned(*units[i])
        if i >= ahead:
            late(*units[i - ahead])
    held = max(len(units) - ahead, 0)
    for i in range(held, min(held + 1, len(units))):
        late(*units[i])
    held = min(held + 1, len(units))

    for k in range(nb):
        local_copy(k).wait()
        core_copy(k).wait_recv()
        for j in range(1, chips):
            for c in range(2):
                y_got(j, c, k, 0).wait_recv()

    packed = packed_rows(total, nz)
    chunk = divisor(share, (64, 32, 16, 8))

    def gather(first):
        x = cells[pl.ds(first, chunk)]
        return jnp.concatenate([x[i] for i in range(chunk)], axis=1)

    mine = row * share

    def gram_body(t, acc):
        x = gather(mine + t * chunk)
        return acc + lax.dot_general(
            x, x, (((1,), (1,)), ((), ())), precision=HIGHEST, preferred_element_type=jnp.float32
        )

    gram = lax.fori_loop(0, share // chunk, gram_body, jnp.zeros((total, total), jnp.float32))
    gram = jnp.concatenate(
        [gram[i * packed:(i + 1) * packed] for i in range(total // packed)], axis=1
    )
    gs[0] = gram
    ar1[me] = gram

    def reduce_1(j):
        return remote(gs.at[0], ar1.at[me], r1_s.at[j - 1], r1_r.at[j - 1], peer_id(j))

    def reduce_2(j):
        return remote(gs.at[1], ar2.at[layer], r2_s.at[j - 1], r2_r.at[j - 1], layer_id(j))

    for j in range(1, group):
        reduce_1(j).start()
    for i in range(held, len(units)):
        late(*units[i])
    for j in range(1, group):
        reduce_1(j).wait_recv()
    total_1 = ar1[0]
    for j in range(1, group):
        total_1 = total_1 + ar1[j]
    gs[1] = total_1
    ar2[layer] = total_1
    for j in range(1, layers):
        reduce_2(j).start()
    for j in range(1, layers):
        reduce_2(j).wait_recv()
    work = ar2[0]
    for j in range(1, layers):
        work = work + ar2[j]

    work = jnp.concatenate(
        [work[:, i * total:(i + 1) * total] for i in range(total // packed)], axis=0
    )
    work = jnp.concatenate([work, jnp.zeros((total, total), jnp.float32)], axis=1)
    lane = lax.broadcasted_iota(jnp.int32, work.shape, 1)
    line = lax.broadcasted_iota(jnp.int32, work.shape, 0)
    work = work / jnp.float32(slab * doms * nz)
    work = jnp.where(lane == line + total, jnp.float32(1.0), work)
    for k in range(total):
        root = jnp.sqrt(work[k:k + 1, k:k + 1])
        scale = 1.0 / root
        pivot = work[k:k + 1, :] * scale
        column = work[:, k:k + 1] * scale
        work = jnp.where(line > k, work - column * pivot, jnp.where(line == k, pivot, work))
    pair = 2 * nb
    for q in range(chips):
        inv[q] = work[q * pair:(q + 1) * pair, total:2 * total]

    pieces = divisor(share // chunk, (4, 3, 2))
    piece = share // pieces

    def give(p, s, k):
        at = pl.multiple_of(((row + p) % chips) * share + s * piece, 8)
        return remote(
            obuf.at[pl.ds(at, piece), 1 - core, k],
            out.at[k, pl.ds(core * part + at, piece)],
            out_s.at[p, s, k], out_r.at[p, s, k], sibling,
        )

    def keep(p, s, k):
        at = pl.multiple_of(((row + p) % chips) * share + s * piece, 8)
        return pltpu.make_async_copy(
            obuf.at[pl.ds(at, piece), core, k],
            out.at[k, pl.ds(core * part + at, piece)], out_l.at[p, s, k],
        )

    for p in range(chips):
        if p > 0:
            for j in range(1, chips):
                @pl.when((row - j + chips) % chips < row)
                def _():
                    for k in range(nb):
                        for c in range(2):
                            y_got(j, c, k, p).wait_recv()
        at_part = ((row + p) % chips) * share

        def piece_body(s, carry):
            def ortho_body(t, carry):
                first = at_part + s * piece + t * chunk
                y = jnp.dot(inv[row], gather(first), precision=HIGH, preferred_element_type=jnp.float32)
                for i in range(chunk):
                    for c in range(2):
                        obuf[first + i, c] = y[c * nb:(c + 1) * nb, i * nz:(i + 1) * nz]
                return carry

            lax.fori_loop(0, piece // chunk, ortho_body, 0)
            for k in range(nb):
                give(p, s, k).start()
                keep(p, s, k).start()
            return carry

        lax.fori_loop(0, pieces, piece_body, 0)

    swap_pot.wait_send()
    for j in range(1, bands):
        pass_pot(j).wait_send()
    for o in range(half):
        for p in range(2):
            swap(o, p).wait_send()
            back(o, p).wait_send()

        @pl.when(has_up)
        def _():
            up(u, o, h1_s, h1_r).wait_send()
            up(f, o, h2_s, h2_r).wait_send()

        @pl.when(has_down)
        def _():
            down(u, o, h1_s, h1_r).wait_send()
            down(f, o, h2_s, h2_r).wait_send()

    for k in range(nb):
        core_copy(k).wait_send()
        for j in range(1, chips):
            for h in range(2):
                y_copy(j, k, h, 0).wait_send()

            @pl.when((row + j) % chips > row)
            def _():
                for h in range(2):
                    for p in range(1, chips):
                        y_copy(j, k, h, p).wait_send()
    for j in range(1, group):
        reduce_1(j).wait_send()
    for j in range(1, layers):
        reduce_2(j).wait_send()
    for p in range(chips):
        for s in range(pieces):
            for k in range(nb):
                keep(p, s, k).wait()
                give(p, s, k).wait()


def deliver(held, out, sem):
    copy = pltpu.make_async_copy(held, out, sem)
    copy.start()
    copy.wait()


def shards(doms, bands, orbitals, potential):
    nb, nx, ny, nz = orbitals.shape
    half = nb // 2
    total = nb * bands
    group = 2 * bands
    layers = doms // 2
    chips = bands // 2
    slab = nx * ny
    part = slab // 2
    share = part // chips
    pair = 2 * nb
    dma = pltpu.SemaphoreType.DMA
    f32 = jnp.float32
    packed = packed_rows(total, nz)
    wide = total * total // packed
    pieces = divisor(share // divisor(share, (64, 32, 16, 8)), (4, 3, 2))
    others = max(chips - 1, 1)
    out = pl.pallas_call(
        functools.partial(kernel, doms, bands, nb, nx, ny, nz),
        out_shape=pltpu.VMEM((nb, slab, nz), f32),
        in_specs=[
            pl.BlockSpec(memory_space=pl.ANY),
            pl.BlockSpec(memory_space=pl.ANY),
        ],
        out_specs=pl.BlockSpec(memory_space=pltpu.VMEM),
        scratch_shapes=[
            pltpu.VMEM((nz, nz), f32),
            pltpu.VMEM((half, 2 * nx + 2 * reach, ny + 2 * pad, nz), f32),
            pltpu.VMEM((half, 2 * nx + 2 * reach, ny + 2 * pad, nz), f32),
            pltpu.VMEM((nb, slab, nz), f32),
            pltpu.VMEM((half, slab, nz), f32),
            pltpu.VMEM((2 * slab, nz), f32),
            pltpu.VMEM((part, total, nz), f32),
            pltpu.VMEM((part, 2, nb, nz), f32),
            pltpu.VMEM((2, packed, wide), f32),
            pltpu.VMEM((group, packed, wide), f32),
            pltpu.VMEM((layers, packed, wide), f32),
            pltpu.VMEM((chips, pair, total), f32),
            dma((half,)),
            dma,
            dma((bands,)),
            dma((bands,)),
            dma((2, half)),
            dma((2, half)),
            dma((2, half)),
            dma((2, half)),
            dma((2, half)),
            dma((2, half)),
            dma((2, half)),
            dma((2, half)),
            dma((nb,)),
            dma((nb,)),
            dma((nb,)),
            dma((others, 2, nb, chips)),
            dma((others, 2, nb, chips)),
            dma((group - 1,)),
            dma((group - 1,)),
            dma((max(layers - 1, 1),)),
            dma((max(layers - 1, 1),)),
            dma((chips, pieces, nb)),
            dma((chips, pieces, nb)),
            dma((chips, pieces, nb)),
        ],
        compiler_params=pltpu.CompilerParams(
            collective_id=0, has_side_effects=True, vmem_limit_bytes=60 * 1024 * 1024
        ),
    )(orbitals, potential.reshape(slab, nz))
    out = pl.pallas_call(
        deliver,
        out_shape=jax.ShapeDtypeStruct((nb, slab, nz), f32),
        in_specs=[pl.BlockSpec(memory_space=pl.ANY)],
        out_specs=pl.BlockSpec(memory_space=pl.ANY),
        scratch_shapes=[dma],
        compiler_params=pltpu.CompilerParams(vmem_limit_bytes=16 * 1024 * 1024),
    )(pltpu.with_memory_space_constraint(out, pltpu.VMEM))
    return out.reshape(orbitals.shape)


def solution(mesh):
    in_specs = (P("band", "dom", None, None), P("dom", None, None))
    out_specs = P("band", "dom", None, None)
    body = functools.partial(shards, mesh.shape["dom"], mesh.shape["band"])
    return jax.shard_map(body, mesh=mesh, in_specs=in_specs, out_specs=out_specs, check_vma=False)
```

```python
import functools
import jax
import jax.numpy as jnp
from jax import lax
from jax.experimental import pallas as pl
from jax.experimental.pallas import tpu as pltpu
from jax.sharding import PartitionSpec as P

stencil_weights = [
    -5369.0 / 1800.0,
    12.0 / 7.0,
    -15.0 / 56.0,
    10.0 / 189.0,
    -1.0 / 112.0,
    2.0 / 1925.0,
    -1.0 / 16632.0,
]
center_shift = 9.5
half_width = 7.5
reach = 6
pad = 8
scaled = [-0.5 * w / half_width for w in stencil_weights]
HIGHEST = lax.Precision.HIGHEST
HIGH = lax.Precision.HIGH
MESH = pl.DeviceIdType.MESH


def divisor(n, options):
    for c in options:
        if n % c == 0:
            return c
    return 1


def packed_rows(total, nz):
    fold = nz // total if total < nz and nz % total == 0 else 1
    return total // fold if total % (8 * fold) == 0 else total


def kernel(
    doms, bands, nb, nx, ny, nz,
    orb, pot, out,
    bz, u, f, own_f, ret_f, potb, cells, obuf, gs, ar1, ar2, inv,
    own_sem, pot_sem, pot_s, pot_r, swap_s, swap_r, h1_s, h1_r, h2_s, h2_r,
    ret_s, ret_r, core_s, core_r, loc_s, y_s, y_r,
    r1_s, r1_r, r2_s, r2_r, out_s, out_r, out_l,
):
    half = nb // 2
    planes = 2 * nx
    total = nb * bands
    group = 2 * bands
    chips = bands // 2
    slab = nx * ny
    part = slab // 2
    share = part // chips
    dom = lax.axis_index("dom")
    band = lax.axis_index("band")
    layer = dom // 2
    layers = doms // 2
    side = dom % 2
    row = band // 2
    core = band % 2
    base = layer * 2
    me = side * bands + band
    partner = {"dom": base + 1 - side, "band": band}
    sibling = {"dom": dom, "band": row * 2 + 1 - core}
    inner, outer = 1 - side, side

    def peer_id(j):
        g = (me + j) % group
        return {"dom": base + g // bands, "band": g % bands}

    def layer_id(j):
        return {"dom": ((layer + j) % layers) * 2 + side, "band": band}

    barrier = pltpu.get_barrier_semaphore()
    for j in range(1, group):
        pl.semaphore_signal(barrier, inc=1, device_id=peer_id(j), device_id_type=MESH)
    for j in range(1, layers):
        pl.semaphore_signal(barrier, inc=1, device_id=layer_id(j), device_id_type=MESH)
    pl.semaphore_wait(barrier, group - 1 + layers - 1)

    def remote(src, dst, s, r, dev):
        return pltpu.make_async_remote_copy(
            src_ref=src, dst_ref=dst, send_sem=s, recv_sem=r, device_id=dev, device_id_type=MESH
        )

    rows = pl.ds(pad, ny)

    def swap(o, p):
        first = (outer if p == 0 else inner) * reach
        return remote(
            orb.at[(1 - side) * half + o, pl.ds(first, reach)],
            u.at[o, pl.ds(reach + side * nx + first, reach), rows],
            swap_s.at[p, o], swap_r.at[p, o], partner,
        )

    pot_share = slab // bands
    pot_rows = pl.ds(pl.multiple_of(band * pot_share, 8), pot_share)
    my_pot = pl.ds(pl.multiple_of(side * slab + band * pot_share, 8), pot_share)
    got_pot = pl.ds(pl.multiple_of((1 - side) * slab + band * pot_share, 8), pot_share)
    swap_pot = remote(pot.at[pot_rows], potb.at[my_pot], pot_s.at[0], pot_r.at[0], partner)

    def pass_pot(j):
        return remote(
            potb.at[got_pot], potb.at[got_pot], pot_s.at[j], pot_r.at[j],
            {"dom": dom, "band": (band + j) % bands},
        )

    def own(o):
        return pltpu.make_async_copy(
            orb.at[side * half + o], u.at[o, pl.ds(reach + side * nx, nx), rows], own_sem.at[o]
        )

    own_pot = pltpu.make_async_copy(
        pot, potb.at[pl.ds(pl.multiple_of(side * slab, 8), slab)], pot_sem
    )

    swap_pot.start()
    for o in range(half):
        for p in range(2):
            swap(o, p).start()
    for o in range(half):
        own(o).start()
    own_pot.start()

    def up(buf, o, s, r):
        return remote(
            buf.at[o, pl.ds(planes, reach), rows], buf.at[o, pl.ds(0, reach), rows],
            s.at[0, o], r.at[0, o], {"dom": dom + 2, "band": band},
        )

    def down(buf, o, s, r):
        return remote(
            buf.at[o, pl.ds(reach, reach), rows], buf.at[o, pl.ds(planes + reach, reach), rows],
            s.at[1, o], r.at[1, o], {"dom": dom - 2, "band": band},
        )

    has_up = layer < layers - 1
    has_down = layer > 0

    def send_face(buf, o, s, r, which):
        @pl.when(jnp.logical_and(has_up, side == which))
        def _():
            up(buf, o, s, r).start()

        @pl.when(jnp.logical_and(has_down, side == 1 - which))
        def _():
            down(buf, o, s, r).start()

    def wait_halos(buf, o, s, r):
        @pl.when(has_down)
        def _():
            up(buf, o, s, r).wait_recv()

        @pl.when(has_up)
        def _():
            down(buf, o, s, r).wait_recv()

    distance = jnp.abs(
        lax.broadcasted_iota(jnp.int32, (nz, nz), 0) - lax.broadcasted_iota(jnp.int32, (nz, nz), 1)
    )
    banded = jnp.zeros((nz, nz), jnp.float32)
    for k in range(1, reach + 1):
        banded = jnp.where(distance == k, jnp.float32(scaled[k]), banded)
    bz[...] = banded
    edge = jnp.zeros((planes + 2 * reach, pad, nz), jnp.float32)
    for buf in (u, f):
        for o in range(half):
            buf[o, :, pl.ds(0, pad), :] = edge
            buf[o, :, pl.ds(pad + ny, pad), :] = edge
    empty = jnp.zeros((reach, ny, nz), jnp.float32)
    for buf in (u, f):
        for o in range(half):
            @pl.when(jnp.logical_not(has_down))
            def _():
                buf[o, pl.ds(0, reach), rows, :] = empty

            @pl.when(jnp.logical_not(has_up))
            def _():
                buf[o, pl.ds(planes + reach, reach), rows, :] = empty

    for q in range(1, chips):
        @pl.when(row < q)
        def _():
            for p in range(1, chips):
                at = ((row + p) % chips) * share
                cells[pl.ds(at, share), pl.ds(q * 2 * nb, 2 * nb), :] = jnp.zeros(
                    (share, 2 * nb, nz), jnp.float32
                )

    def apply(buf, o, first, count, emit):
        step = divisor(count, (4, 3, 2))

        def body(t, carry):
            x0 = first + t * step
            centre = [buf[o, reach + x0 + i, pl.ds(pad, ny), :] for i in range(step)]
            along_z = jnp.dot(
                jnp.concatenate(centre, axis=0), bz[...], precision=HIGHEST,
                preferred_element_type=jnp.float32,
            )
            for i in range(step):
                x = reach + x0 + i
                weight = potb[pl.ds(pl.multiple_of((x0 + i) * ny, 8), ny), :] * (1.0 / half_width) + (
                    3.0 * scaled[0] - center_shift / half_width
                )
                acc = along_z[i * ny:(i + 1) * ny] + weight * centre[i]
                for k in range(1, reach + 1):
                    near = buf[o, x + k, pl.ds(pad, ny), :] + buf[o, x - k, pl.ds(pad, ny), :]
                    near = near + (
                        buf[o, x, pl.ds(pad + k, ny), :] + buf[o, x, pl.ds(pad - k, ny), :]
                    )
                    acc = acc + scaled[k] * near
                emit(x0 + i, acc)
            return carry

        lax.fori_loop(0, count // step, body, 0)

    def first_term(o, first, count):
        def emit(x, acc):
            f[o, reach + x, pl.ds(pad, ny), :] = acc

        apply(u, o, first, count, emit)

    def second_term(o, slab_side, which, dst, k):
        def emit(x, acc):
            start = pl.multiple_of((x - slab_side * nx) * ny, 8)
            dst[k, pl.ds(start, ny), :] = 2.0 * acc - u[o, reach + x, pl.ds(pad, ny), :]

        apply(f, o, slab_side * nx + which * reach, reach, emit)

    def y_copy(j, k, h, p):
        to = (row + j) % chips
        at = ((to + p) % chips) * share
        return remote(
            own_f.at[k, pl.ds(pl.multiple_of(h * part + at, 8), share)],
            cells.at[pl.ds(at, share), band * nb + k],
            y_s.at[j - 1, h, k, p], y_r.at[j - 1, core, k, p],
            {"dom": dom, "band": to * 2 + h},
        )

    def y_got(j, c, k, p):
        to = row
        at = ((to + p) % chips) * share
        from_band = ((row - j + chips) % chips) * 2 + c
        return remote(
            own_f.at[k, pl.ds(pl.multiple_of(at, 8), share)],
            cells.at[pl.ds(at, share), from_band * nb + k],
            y_s.at[j - 1, 0, k, p], y_r.at[j - 1, c, k, p],
            {"dom": dom, "band": ((row + j) % chips) * 2},
        )

    def core_copy(k):
        return remote(
            own_f.at[k, pl.ds(pl.multiple_of((1 - core) * part, 8), part)],
            cells.at[:, band * nb + k],
            core_s.at[k], core_r.at[k], sibling,
        )

    def local_copy(k):
        return pltpu.make_async_copy(
            own_f.at[k, pl.ds(pl.multiple_of(core * part, 8), part)],
            cells.at[:, band * nb + k],
            loc_s.at[k],
        )

    def spread(k, h):
        for j in range(1, chips):
            y_copy(j, k, h, 0).start()
        spread_chip(k, h)

    def spread_chip(k, h):
        @pl.when(h != core)
        def _():
            core_copy(k).start()

        @pl.when(h == core)
        def _():
            local_copy(k).start()

    def spread_rest(k, h):
        for j in range(1, chips):
            @pl.when((row + j) % chips > row)
            def _():
                for p in range(1, chips):
                    y_copy(j, k, h, p).start()

    def piece_of(h, q):
        return pl.ds(pl.multiple_of(h * part + ((row + q) % chips) * share, 8), share)

    def back(o, h, q):
        at = piece_of(h, q)
        return remote(
            ret_f.at[o, at], own_f.at[side * half + o, at], ret_s.at[h, o, q], ret_r.at[h, o, q], partner
        )

    def came(o, h, q):
        at = piece_of(h, q)
        return remote(
            ret_f.at[o, at], own_f.at[(1 - side) * half + o, at], ret_s.at[h, o, q], ret_r.at[h, o, q],
            partner,
        )

    def finish(o, which):
        k = side * half + o
        second_term(o, side, which, own_f, k)
        spread(k, which)
        spread_rest(k, which)
        second_term(o, 1 - side, 1 - which, ret_f, o)
        for q in range(1, chips + 1):
            back(o, 1 - which, q % chips).start()

    def returned(o, which):
        k = (1 - side) * half + o
        for q in range(1, chips):
            came(o, which, q).wait_recv()
            y_copy(q, k, which, 0).start()
        came(o, which, 0).wait_recv()
        spread_chip(k, which)

    def late(o, which):
        spread_rest((1 - side) * half + o, which)

    swap_pot.wait_recv()
    for j in range(1, bands):
        pass_pot(j).start()
    for o in range(min(2, half)):
        own(o).wait()
        send_face(u, o, h1_s, h1_r, 1)
    own_pot.wait()

    for o in range(half):
        swap(o, 0).wait_recv()
        send_face(u, o, h1_s, h1_r, 0)
        if o == 0:
            for j in range(1, bands):
                pass_pot(j).wait_recv()
        swap(o, 1).wait_recv()
        first_term(o, reach, planes - 2 * reach)
        if o > 0:
            wait_halos(f, o - 1, h2_s, h2_r)
            finish(o - 1, outer)
        wait_halos(u, o, h1_s, h1_r)
        first_term(o, 0, reach)
        first_term(o, planes - reach, reach)
        send_face(f, o, h2_s, h2_r, 1)
        send_face(f, o, h2_s, h2_r, 0)
        if o + 2 < half:
            own(o + 2).wait()
            send_face(u, o + 2, h1_s, h1_r, 1)
        finish(o, inner)
    units = [(o, w) for o in range(half) for w in (inner, outer)]
    ahead = 6
    returned(*units[0])
    wait_halos(f, half - 1, h2_s, h2_r)
    finish(half - 1, outer)
    for i in range(1, len(units)):
        returned(*units[i])
        if i >= ahead:
            late(*units[i - ahead])
    held = max(len(units) - ahead, 0)

    for k in range(nb):
        local_copy(k).wait()
        core_copy(k).wait_recv()
        for j in range(1, chips):
            for c in range(2):
                y_got(j, c, k, 0).wait_recv()

    packed = packed_rows(total, nz)
    chunk = divisor(share, (64, 32, 16, 8))

    def gather(first):
        x = cells[pl.ds(first, chunk)]
        return jnp.concatenate([x[i] for i in range(chunk)], axis=1)

    mine = row * share

    def gram_body(t, acc):
        x = gather(mine + t * chunk)
        return acc + lax.dot_general(
            x, x, (((1,), (1,)), ((), ())), precision=HIGH, preferred_element_type=jnp.float32
        )

    gram = lax.fori_loop(0, share // chunk, gram_body, jnp.zeros((total, total), jnp.float32))
    gram = jnp.concatenate(
        [gram[i * packed:(i + 1) * packed] for i in range(total // packed)], axis=1
    )
    gs[0] = gram
    ar1[me] = gram

    def reduce_1(j):
        return remote(gs.at[0], ar1.at[me], r1_s.at[j - 1], r1_r.at[j - 1], peer_id(j))

    def reduce_2(j):
        return remote(gs.at[1], ar2.at[layer], r2_s.at[j - 1], r2_r.at[j - 1], layer_id(j))

    for j in range(1, group):
        reduce_1(j).start()
    for i in range(held, len(units)):
        late(*units[i])
    for j in range(1, group):
        reduce_1(j).wait_recv()
    total_1 = ar1[0]
    for j in range(1, group):
        total_1 = total_1 + ar1[j]
    gs[1] = total_1
    ar2[layer] = total_1
    for j in range(1, layers):
        reduce_2(j).start()
    for j in range(1, layers):
        reduce_2(j).wait_recv()
    work = ar2[0]
    for j in range(1, layers):
        work = work + ar2[j]

    work = jnp.concatenate(
        [work[:, i * total:(i + 1) * total] for i in range(total // packed)], axis=0
    )
    work = jnp.concatenate([work, jnp.zeros((total, total), jnp.float32)], axis=1)
    lane = lax.broadcasted_iota(jnp.int32, work.shape, 1)
    line = lax.broadcasted_iota(jnp.int32, work.shape, 0)
    work = work / jnp.float32(slab * doms * nz)
    work = jnp.where(lane == line + total, jnp.float32(1.0), work)
    for k in range(total):
        root = jnp.sqrt(work[k:k + 1, k:k + 1])
        scale = 1.0 / root
        pivot = work[k:k + 1, :] * scale
        column = work[:, k:k + 1] * scale
        work = jnp.where(line > k, work - column * pivot, jnp.where(line == k, pivot, work))
    pair = 2 * nb
    for q in range(chips):
        inv[q] = work[q * pair:(q + 1) * pair, total:2 * total]

    pieces = 1
    piece = share // pieces

    def give(p, s, k):
        at = pl.multiple_of(((row + p) % chips) * share + s * piece, 8)
        return remote(
            obuf.at[pl.ds(at, piece), 1 - core, k],
            out.at[k, pl.ds(core * part + at, piece)],
            out_s.at[p, s, k], out_r.at[p, s, k], sibling,
        )

    def keep(p, s, k):
        at = pl.multiple_of(((row + p) % chips) * share + s * piece, 8)
        return pltpu.make_async_copy(
            obuf.at[pl.ds(at, piece), core, k],
            out.at[k, pl.ds(core * part + at, piece)], out_l.at[p, s, k],
        )

    for p in range(chips):
        if p > 0:
            for j in range(1, chips):
                @pl.when((row - j + chips) % chips < row)
                def _():
                    for k in range(nb):
                        for c in range(2):
                            y_got(j, c, k, p).wait_recv()
        at_part = ((row + p) % chips) * share

        def piece_body(s, carry):
            def ortho_body(t, carry):
                first = at_part + s * piece + t * chunk
                y = jnp.dot(inv[row], gather(first), precision=HIGH, preferred_element_type=jnp.float32)
                for i in range(chunk):
                    for c in range(2):
                        obuf[first + i, c] = y[c * nb:(c + 1) * nb, i * nz:(i + 1) * nz]
                return carry

            lax.fori_loop(0, piece // chunk, ortho_body, 0)
            for k in range(nb):
                give(p, s, k).start()
                keep(p, s, k).start()
            return carry

        lax.fori_loop(0, pieces, piece_body, 0)

    swap_pot.wait_send()
    for j in range(1, bands):
        pass_pot(j).wait_send()
    for o in range(half):
        for p in range(2):
            swap(o, p).wait_send()
            for q in range(chips):
                back(o, p, q).wait_send()

        @pl.when(has_up)
        def _():
            up(u, o, h1_s, h1_r).wait_send()
            up(f, o, h2_s, h2_r).wait_send()

        @pl.when(has_down)
        def _():
            down(u, o, h1_s, h1_r).wait_send()
            down(f, o, h2_s, h2_r).wait_send()

    for k in range(nb):
        core_copy(k).wait_send()
        for j in range(1, chips):
            for h in range(2):
                y_copy(j, k, h, 0).wait_send()

            @pl.when((row + j) % chips > row)
            def _():
                for h in range(2):
                    for p in range(1, chips):
                        y_copy(j, k, h, p).wait_send()
    for j in range(1, group):
        reduce_1(j).wait_send()
    for j in range(1, layers):
        reduce_2(j).wait_send()
    for p in range(chips):
        for s in range(pieces):
            for k in range(nb):
                keep(p, s, k).wait()
                give(p, s, k).wait()


def deliver(held, out, sem):
    copy = pltpu.make_async_copy(held, out, sem)
    copy.start()
    copy.wait()


def shards(doms, bands, orbitals, potential):
    nb, nx, ny, nz = orbitals.shape
    half = nb // 2
    total = nb * bands
    group = 2 * bands
    layers = doms // 2
    chips = bands // 2
    slab = nx * ny
    part = slab // 2
    share = part // chips
    pair = 2 * nb
    dma = pltpu.SemaphoreType.DMA
    f32 = jnp.float32
    packed = packed_rows(total, nz)
    wide = total * total // packed
    pieces = 1
    others = max(chips - 1, 1)
    out = pl.pallas_call(
        functools.partial(kernel, doms, bands, nb, nx, ny, nz),
        out_shape=pltpu.VMEM((nb, slab, nz), f32),
        in_specs=[
            pl.BlockSpec(memory_space=pl.ANY),
            pl.BlockSpec(memory_space=pl.ANY),
        ],
        out_specs=pl.BlockSpec(memory_space=pltpu.VMEM),
        scratch_shapes=[
            pltpu.VMEM((nz, nz), f32),
            pltpu.VMEM((half, 2 * nx + 2 * reach, ny + 2 * pad, nz), f32),
            pltpu.VMEM((half, 2 * nx + 2 * reach, ny + 2 * pad, nz), f32),
            pltpu.VMEM((nb, slab, nz), f32),
            pltpu.VMEM((half, slab, nz), f32),
            pltpu.VMEM((2 * slab, nz), f32),
            pltpu.VMEM((part, total, nz), f32),
            pltpu.VMEM((part, 2, nb, nz), f32),
            pltpu.VMEM((2, packed, wide), f32),
            pltpu.VMEM((group, packed, wide), f32),
            pltpu.VMEM((layers, packed, wide), f32),
            pltpu.VMEM((chips, pair, total), f32),
            dma((half,)),
            dma,
            dma((bands,)),
            dma((bands,)),
            dma((2, half)),
            dma((2, half)),
            dma((2, half)),
            dma((2, half)),
            dma((2, half)),
            dma((2, half)),
            dma((2, half, chips)),
            dma((2, half, chips)),
            dma((nb,)),
            dma((nb,)),
            dma((nb,)),
            dma((others, 2, nb, chips)),
            dma((others, 2, nb, chips)),
            dma((group - 1,)),
            dma((group - 1,)),
            dma((max(layers - 1, 1),)),
            dma((max(layers - 1, 1),)),
            dma((chips, pieces, nb)),
            dma((chips, pieces, nb)),
            dma((chips, pieces, nb)),
        ],
        compiler_params=pltpu.CompilerParams(
            collective_id=0, has_side_effects=True, vmem_limit_bytes=60 * 1024 * 1024
        ),
    )(orbitals, potential.reshape(slab, nz))
    out = pl.pallas_call(
        deliver,
        out_shape=jax.ShapeDtypeStruct((nb, slab, nz), f32),
        in_specs=[pl.BlockSpec(memory_space=pl.ANY)],
        out_specs=pl.BlockSpec(memory_space=pl.ANY),
        scratch_shapes=[dma],
        compiler_params=pltpu.CompilerParams(vmem_limit_bytes=16 * 1024 * 1024),
    )(pltpu.with_memory_space_constraint(out, pltpu.VMEM))
    return out.reshape(orbitals.shape)


def solution(mesh):
    in_specs = (P("band", "dom", None, None), P("dom", None, None))
    out_specs = P("band", "dom", None, None)
    body = functools.partial(shards, mesh.shape["dom"], mesh.shape["band"])
    return jax.shard_map(body, mesh=mesh, in_specs=in_specs, out_specs=out_specs, check_vma=False)
```

```python
import functools
import jax
import jax.numpy as jnp
from jax import lax
from jax.experimental import pallas as pl
from jax.experimental.pallas import tpu as pltpu
from jax.sharding import PartitionSpec as P

stencil_weights = [
    -5369.0 / 1800.0,
    12.0 / 7.0,
    -15.0 / 56.0,
    10.0 / 189.0,
    -1.0 / 112.0,
    2.0 / 1925.0,
    -1.0 / 16632.0,
]
center_shift = 9.5
half_width = 7.5
reach = 6
pad = 8
scaled = [-0.5 * w / half_width for w in stencil_weights]
HIGHEST = lax.Precision.HIGHEST
HIGH = lax.Precision.HIGH
MESH = pl.DeviceIdType.MESH


def divisor(n, options):
    for c in options:
        if n % c == 0:
            return c
    return 1


def packed_rows(total, nz):
    fold = nz // total if total < nz and nz % total == 0 else 1
    return total // fold if total % (8 * fold) == 0 else total


def kernel(
    doms, bands, nb, nx, ny, nz,
    orb, pot, out,
    bz, u, f, own_f, ret_f, potb, cells, obuf, gs, ar1, ar2, inv,
    own_sem, pot_sem, pot_s, pot_r, swap_s, swap_r, h1_s, h1_r, h2_s, h2_r,
    ret_s, ret_r, core_s, core_r, loc_s, y_s, y_r,
    r1_s, r1_r, r2_s, r2_r, out_s, out_r, out_l,
):
    half = nb // 2
    planes = 2 * nx
    total = nb * bands
    group = 2 * bands
    chips = bands // 2
    slab = nx * ny
    part = slab // 2
    share = part // chips
    dom = lax.axis_index("dom")
    band = lax.axis_index("band")
    layer = dom // 2
    layers = doms // 2
    side = dom % 2
    row = band // 2
    core = band % 2
    base = layer * 2
    me = side * bands + band
    partner = {"dom": base + 1 - side, "band": band}
    sibling = {"dom": dom, "band": row * 2 + 1 - core}
    inner, outer = 1 - side, side

    def peer_id(j):
        g = (me + j) % group
        return {"dom": base + g // bands, "band": g % bands}

    def layer_id(j):
        return {"dom": ((layer + j) % layers) * 2 + side, "band": band}

    barrier = pltpu.get_barrier_semaphore()
    for j in range(1, group):
        pl.semaphore_signal(barrier, inc=1, device_id=peer_id(j), device_id_type=MESH)
    for j in range(1, layers):
        pl.semaphore_signal(barrier, inc=1, device_id=layer_id(j), device_id_type=MESH)
    pl.semaphore_wait(barrier, group - 1 + layers - 1)

    def remote(src, dst, s, r, dev):
        return pltpu.make_async_remote_copy(
            src_ref=src, dst_ref=dst, send_sem=s, recv_sem=r, device_id=dev, device_id_type=MESH
        )

    rows = pl.ds(pad, ny)

    def swap(o, p):
        first = (outer if p == 0 else inner) * reach
        return remote(
            orb.at[(1 - side) * half + o, pl.ds(first, reach)],
            u.at[o, pl.ds(reach + side * nx + first, reach), rows],
            swap_s.at[p, o], swap_r.at[p, o], partner,
        )

    pot_share = slab // bands
    pot_rows = pl.ds(pl.multiple_of(band * pot_share, 8), pot_share)
    my_pot = pl.ds(pl.multiple_of(side * slab + band * pot_share, 8), pot_share)
    got_pot = pl.ds(pl.multiple_of((1 - side) * slab + band * pot_share, 8), pot_share)
    swap_pot = remote(pot.at[pot_rows], potb.at[my_pot], pot_s.at[0], pot_r.at[0], partner)

    def pass_pot(j):
        return remote(
            potb.at[got_pot], potb.at[got_pot], pot_s.at[j], pot_r.at[j],
            {"dom": dom, "band": (band + j) % bands},
        )

    def own(o):
        return pltpu.make_async_copy(
            orb.at[side * half + o], u.at[o, pl.ds(reach + side * nx, nx), rows], own_sem.at[o]
        )

    own_pot = pltpu.make_async_copy(
        pot, potb.at[pl.ds(pl.multiple_of(side * slab, 8), slab)], pot_sem
    )

    swap_pot.start()
    for o in range(half):
        for p in range(2):
            swap(o, p).start()
    for o in range(half):
        own(o).start()
    own_pot.start()

    def up(buf, o, s, r):
        return remote(
            buf.at[o, pl.ds(planes, reach), rows], buf.at[o, pl.ds(0, reach), rows],
            s.at[0, o], r.at[0, o], {"dom": dom + 2, "band": band},
        )

    def down(buf, o, s, r):
        return remote(
            buf.at[o, pl.ds(reach, reach), rows], buf.at[o, pl.ds(planes + reach, reach), rows],
            s.at[1, o], r.at[1, o], {"dom": dom - 2, "band": band},
        )

    has_up = layer < layers - 1
    has_down = layer > 0

    def send_face(buf, o, s, r, which):
        @pl.when(jnp.logical_and(has_up, side == which))
        def _():
            up(buf, o, s, r).start()

        @pl.when(jnp.logical_and(has_down, side == 1 - which))
        def _():
            down(buf, o, s, r).start()

    def wait_halos(buf, o, s, r):
        @pl.when(has_down)
        def _():
            up(buf, o, s, r).wait_recv()

        @pl.when(has_up)
        def _():
            down(buf, o, s, r).wait_recv()

    distance = jnp.abs(
        lax.broadcasted_iota(jnp.int32, (nz, nz), 0) - lax.broadcasted_iota(jnp.int32, (nz, nz), 1)
    )
    banded = jnp.zeros((nz, nz), jnp.float32)
    for k in range(1, reach + 1):
        banded = jnp.where(distance == k, jnp.float32(scaled[k]), banded)
    bz[...] = banded
    edge = jnp.zeros((planes + 2 * reach, pad, nz), jnp.float32)
    for buf in (u, f):
        for o in range(half):
            buf[o, :, pl.ds(0, pad), :] = edge
            buf[o, :, pl.ds(pad + ny, pad), :] = edge
    empty = jnp.zeros((reach, ny, nz), jnp.float32)
    for buf in (u, f):
        for o in range(half):
            @pl.when(jnp.logical_not(has_down))
            def _():
                buf[o, pl.ds(0, reach), rows, :] = empty

            @pl.when(jnp.logical_not(has_up))
            def _():
                buf[o, pl.ds(planes + reach, reach), rows, :] = empty

    for q in range(1, chips):
        @pl.when(row < q)
        def _():
            for p in range(1, chips):
                at = ((row + p) % chips) * share
                cells[pl.ds(at, share), pl.ds(q * 2 * nb, 2 * nb), :] = jnp.zeros(
                    (share, 2 * nb, nz), jnp.float32
                )

    def apply(buf, o, first, count, emit):
        step = divisor(count, (4, 3, 2))

        def body(t, carry):
            x0 = first + t * step
            centre = [buf[o, reach + x0 + i, pl.ds(pad, ny), :] for i in range(step)]
            along_z = jnp.dot(
                jnp.concatenate(centre, axis=0), bz[...], precision=HIGHEST,
                preferred_element_type=jnp.float32,
            )
            for i in range(step):
                x = reach + x0 + i
                weight = potb[pl.ds(pl.multiple_of((x0 + i) * ny, 8), ny), :] * (1.0 / half_width) + (
                    3.0 * scaled[0] - center_shift / half_width
                )
                acc = along_z[i * ny:(i + 1) * ny] + weight * centre[i]
                for k in range(1, reach + 1):
                    near = buf[o, x + k, pl.ds(pad, ny), :] + buf[o, x - k, pl.ds(pad, ny), :]
                    near = near + (
                        buf[o, x, pl.ds(pad + k, ny), :] + buf[o, x, pl.ds(pad - k, ny), :]
                    )
                    acc = acc + scaled[k] * near
                emit(x0 + i, acc)
            return carry

        lax.fori_loop(0, count // step, body, 0)

    def first_term(o, first, count):
        def emit(x, acc):
            f[o, reach + x, pl.ds(pad, ny), :] = acc

        apply(u, o, first, count, emit)

    def second_term(o, slab_side, which, dst, k):
        def emit(x, acc):
            start = pl.multiple_of((x - slab_side * nx) * ny, 8)
            dst[k, pl.ds(start, ny), :] = 2.0 * acc - u[o, reach + x, pl.ds(pad, ny), :]

        apply(f, o, slab_side * nx + which * reach, reach, emit)

    def y_copy(j, k, h, p):
        to = (row + j) % chips
        at = ((to + p) % chips) * share
        return remote(
            own_f.at[k, pl.ds(pl.multiple_of(h * part + at, 8), share)],
            cells.at[pl.ds(at, share), band * nb + k],
            y_s.at[j - 1, h, k, p], y_r.at[j - 1, core, k, p],
            {"dom": dom, "band": to * 2 + h},
        )

    def y_got(j, c, k, p):
        to = row
        at = ((to + p) % chips) * share
        from_band = ((row - j + chips) % chips) * 2 + c
        return remote(
            own_f.at[k, pl.ds(pl.multiple_of(at, 8), share)],
            cells.at[pl.ds(at, share), from_band * nb + k],
            y_s.at[j - 1, 0, k, p], y_r.at[j - 1, c, k, p],
            {"dom": dom, "band": ((row + j) % chips) * 2},
        )

    def core_copy(k):
        return remote(
            own_f.at[k, pl.ds(pl.multiple_of((1 - core) * part, 8), part)],
            cells.at[:, band * nb + k],
            core_s.at[k], core_r.at[k], sibling,
        )

    def local_copy(k):
        return pltpu.make_async_copy(
            own_f.at[k, pl.ds(pl.multiple_of(core * part, 8), part)],
            cells.at[:, band * nb + k],
            loc_s.at[k],
        )

    def spread(k, h):
        for j in range(1, chips):
            y_copy(j, k, h, 0).start()
        spread_chip(k, h)

    def spread_chip(k, h):
        @pl.when(h != core)
        def _():
            core_copy(k).start()

        @pl.when(h == core)
        def _():
            local_copy(k).start()

    def spread_rest(k, h):
        for j in range(1, chips):
            @pl.when((row + j) % chips > row)
            def _():
                for p in range(1, chips):
                    y_copy(j, k, h, p).start()

    def piece_of(h, q):
        return pl.ds(pl.multiple_of(h * part + ((row + q) % chips) * share, 8), share)

    def back(o, h, q):
        at = piece_of(h, q)
        return remote(
            ret_f.at[o, at], own_f.at[side * half + o, at], ret_s.at[h, o, q], ret_r.at[h, o, q], partner
        )

    def came(o, h, q):
        at = piece_of(h, q)
        return remote(
            ret_f.at[o, at], own_f.at[(1 - side) * half + o, at], ret_s.at[h, o, q], ret_r.at[h, o, q],
            partner,
        )

    def finish(o, which):
        k = side * half + o
        second_term(o, side, which, own_f, k)
        spread(k, which)
        spread_rest(k, which)
        second_term(o, 1 - side, 1 - which, ret_f, o)
        for q in range(1, chips + 1):
            back(o, 1 - which, q % chips).start()

    def returned(o, which):
        k = (1 - side) * half + o
        for q in range(1, chips):
            came(o, which, q).wait_recv()
            y_copy(q, k, which, 0).start()
        came(o, which, 0).wait_recv()
        spread_chip(k, which)

    def late(o, which):
        spread_rest((1 - side) * half + o, which)

    swap_pot.wait_recv()
    for j in range(1, bands):
        pass_pot(j).start()
    for o in range(min(2, half)):
        own(o).wait()
        send_face(u, o, h1_s, h1_r, 1)
    own_pot.wait()

    for o in range(half):
        swap(o, 0).wait_recv()
        send_face(u, o, h1_s, h1_r, 0)
        if o == 0:
            for j in range(1, bands):
                pass_pot(j).wait_recv()
        swap(o, 1).wait_recv()
        first_term(o, reach, planes - 2 * reach)
        if o > 0:
            wait_halos(f, o - 1, h2_s, h2_r)
            finish(o - 1, outer)
        wait_halos(u, o, h1_s, h1_r)
        first_term(o, 0, reach)
        first_term(o, planes - reach, reach)
        send_face(f, o, h2_s, h2_r, 1)
        send_face(f, o, h2_s, h2_r, 0)
        if o + 2 < half:
            own(o + 2).wait()
            send_face(u, o + 2, h1_s, h1_r, 1)
        finish(o, inner)
    units = [(o, w) for o in range(half) for w in (inner, outer)]
    ahead = 6
    returned(*units[0])
    wait_halos(f, half - 1, h2_s, h2_r)
    finish(half - 1, outer)
    for i in range(1, len(units)):
        returned(*units[i])
        if i >= ahead:
            late(*units[i - ahead])
    held = max(len(units) - ahead, 0)

    for k in range(nb):
        local_copy(k).wait()
        core_copy(k).wait_recv()
        for j in range(1, chips):
            for c in range(2):
                y_got(j, c, k, 0).wait_recv()

    packed = packed_rows(total, nz)
    chunk = divisor(share, (96, 64, 32, 16, 8))

    def gather(first):
        x = cells[pl.ds(first, chunk)]
        return jnp.concatenate([x[i] for i in range(chunk)], axis=1)

    mine = row * share

    def gram_body(t, acc):
        x = gather(mine + t * chunk)
        return acc + lax.dot_general(
            x, x, (((1,), (1,)), ((), ())), precision=HIGH, preferred_element_type=jnp.float32
        )

    gram = lax.fori_loop(0, share // chunk, gram_body, jnp.zeros((total, total), jnp.float32))
    gram = jnp.concatenate(
        [gram[i * packed:(i + 1) * packed] for i in range(total // packed)], axis=1
    )
    gs[0] = gram
    ar1[me] = gram

    def reduce_1(j):
        return remote(gs.at[0], ar1.at[me], r1_s.at[j - 1], r1_r.at[j - 1], peer_id(j))

    def reduce_2(j):
        return remote(gs.at[1], ar2.at[layer], r2_s.at[j - 1], r2_r.at[j - 1], layer_id(j))

    for j in range(1, group):
        reduce_1(j).start()
    for i in range(held, len(units)):
        late(*units[i])
    swap_pot.wait_send()
    for j in range(1, bands):
        pass_pot(j).wait_send()
    for o in range(half):
        for p in range(2):
            swap(o, p).wait_send()
            for q in range(chips):
                back(o, p, q).wait_send()

        @pl.when(has_up)
        def _():
            up(u, o, h1_s, h1_r).wait_send()
            up(f, o, h2_s, h2_r).wait_send()

        @pl.when(has_down)
        def _():
            down(u, o, h1_s, h1_r).wait_send()
            down(f, o, h2_s, h2_r).wait_send()

    for k in range(nb):
        core_copy(k).wait_send()
        for j in range(1, chips):
            for h in range(2):
                y_copy(j, k, h, 0).wait_send()
    for j in range(1, group):
        reduce_1(j).wait_recv()
    total_1 = ar1[0]
    for j in range(1, group):
        total_1 = total_1 + ar1[j]
    gs[1] = total_1
    ar2[layer] = total_1
    for j in range(1, layers):
        reduce_2(j).start()
    for j in range(1, layers):
        reduce_2(j).wait_recv()
    work = ar2[0]
    for j in range(1, layers):
        work = work + ar2[j]

    work = jnp.concatenate(
        [work[:, i * total:(i + 1) * total] for i in range(total // packed)], axis=0
    )
    work = jnp.concatenate([work, jnp.zeros((total, total), jnp.float32)], axis=1)
    lane = lax.broadcasted_iota(jnp.int32, work.shape, 1)
    line = lax.broadcasted_iota(jnp.int32, work.shape, 0)
    work = work / jnp.float32(slab * doms * nz)
    work = jnp.where(lane == line + total, jnp.float32(1.0), work)
    for k in range(total):
        root = jnp.sqrt(work[k:k + 1, k:k + 1])
        scale = 1.0 / root
        pivot = work[k:k + 1, :] * scale
        column = work[:, k:k + 1] * scale
        work = jnp.where(line > k, work - column * pivot, jnp.where(line == k, pivot, work))
    pair = 2 * nb
    for q in range(chips):
        inv[q] = work[q * pair:(q + 1) * pair, total:2 * total]

    pieces = 1
    piece = share // pieces

    def give(p, s, k):
        at = pl.multiple_of(((row + p) % chips) * share + s * piece, 8)
        return remote(
            obuf.at[pl.ds(at, piece), 1 - core, k],
            out.at[k, pl.ds(core * part + at, piece)],
            out_s.at[p, s, k], out_r.at[p, s, k], sibling,
        )

    def keep(p, s, k):
        at = pl.multiple_of(((row + p) % chips) * share + s * piece, 8)
        return pltpu.make_async_copy(
            obuf.at[pl.ds(at, piece), core, k],
            out.at[k, pl.ds(core * part + at, piece)], out_l.at[p, s, k],
        )

    for p in range(chips):
        if p > 0:
            for j in range(1, chips):
                @pl.when((row - j + chips) % chips < row)
                def _():
                    for k in range(nb):
                        for c in range(2):
                            y_got(j, c, k, p).wait_recv()
        at_part = ((row + p) % chips) * share

        def piece_body(s, carry):
            def ortho_body(t, carry):
                first = at_part + s * piece + t * chunk
                y = jnp.dot(inv[row], gather(first), precision=HIGH, preferred_element_type=jnp.float32)
                for i in range(chunk):
                    for c in range(2):
                        obuf[first + i, c] = y[c * nb:(c + 1) * nb, i * nz:(i + 1) * nz]
                return carry

            lax.fori_loop(0, piece // chunk, ortho_body, 0)
            for k in range(nb):
                give(p, s, k).start()
                keep(p, s, k).start()
            return carry

        lax.fori_loop(0, pieces, piece_body, 0)

    for k in range(nb):
        for j in range(1, chips):
            @pl.when((row + j) % chips > row)
            def _():
                for h in range(2):
                    for p in range(1, chips):
                        y_copy(j, k, h, p).wait_send()
    for j in range(1, group):
        reduce_1(j).wait_send()
    for j in range(1, layers):
        reduce_2(j).wait_send()
    for p in range(chips):
        for s in range(pieces):
            for k in range(nb):
                keep(p, s, k).wait()
                give(p, s, k).wait()


def deliver(held, out, sem):
    copy = pltpu.make_async_copy(held, out, sem)
    copy.start()
    copy.wait()


def shards(doms, bands, orbitals, potential):
    nb, nx, ny, nz = orbitals.shape
    half = nb // 2
    total = nb * bands
    group = 2 * bands
    layers = doms // 2
    chips = bands // 2
    slab = nx * ny
    part = slab // 2
    share = part // chips
    pair = 2 * nb
    dma = pltpu.SemaphoreType.DMA
    f32 = jnp.float32
    packed = packed_rows(total, nz)
    wide = total * total // packed
    pieces = 1
    others = max(chips - 1, 1)
    out = pl.pallas_call(
        functools.partial(kernel, doms, bands, nb, nx, ny, nz),
        out_shape=pltpu.VMEM((nb, slab, nz), f32),
        in_specs=[
            pl.BlockSpec(memory_space=pl.ANY),
            pl.BlockSpec(memory_space=pl.ANY),
        ],
        out_specs=pl.BlockSpec(memory_space=pltpu.VMEM),
        scratch_shapes=[
            pltpu.VMEM((nz, nz), f32),
            pltpu.VMEM((half, 2 * nx + 2 * reach, ny + 2 * pad, nz), f32),
            pltpu.VMEM((half, 2 * nx + 2 * reach, ny + 2 * pad, nz), f32),
            pltpu.VMEM((nb, slab, nz), f32),
            pltpu.VMEM((half, slab, nz), f32),
            pltpu.VMEM((2 * slab, nz), f32),
            pltpu.VMEM((part, total, nz), f32),
            pltpu.VMEM((part, 2, nb, nz), f32),
            pltpu.VMEM((2, packed, wide), f32),
            pltpu.VMEM((group, packed, wide), f32),
            pltpu.VMEM((layers, packed, wide), f32),
            pltpu.VMEM((chips, pair, total), f32),
            dma((half,)),
            dma,
            dma((bands,)),
            dma((bands,)),
            dma((2, half)),
            dma((2, half)),
            dma((2, half)),
            dma((2, half)),
            dma((2, half)),
            dma((2, half)),
            dma((2, half, chips)),
            dma((2, half, chips)),
            dma((nb,)),
            dma((nb,)),
            dma((nb,)),
            dma((others, 2, nb, chips)),
            dma((others, 2, nb, chips)),
            dma((group - 1,)),
            dma((group - 1,)),
            dma((max(layers - 1, 1),)),
            dma((max(layers - 1, 1),)),
            dma((chips, pieces, nb)),
            dma((chips, pieces, nb)),
            dma((chips, pieces, nb)),
        ],
        compiler_params=pltpu.CompilerParams(
            collective_id=0, has_side_effects=True, vmem_limit_bytes=60 * 1024 * 1024
        ),
    )(orbitals, potential.reshape(slab, nz))
    out = pl.pallas_call(
        deliver,
        out_shape=jax.ShapeDtypeStruct((nb, slab, nz), f32),
        in_specs=[pl.BlockSpec(memory_space=pl.ANY)],
        out_specs=pl.BlockSpec(memory_space=pl.ANY),
        scratch_shapes=[dma],
        compiler_params=pltpu.CompilerParams(vmem_limit_bytes=16 * 1024 * 1024),
    )(pltpu.with_memory_space_constraint(out, pltpu.VMEM))
    return out.reshape(orbitals.shape)


def solution(mesh):
    in_specs = (P("band", "dom", None, None), P("dom", None, None))
    out_specs = P("band", "dom", None, None)
    body = functools.partial(shards, mesh.shape["dom"], mesh.shape["band"])
    return jax.shard_map(body, mesh=mesh, in_specs=in_specs, out_specs=out_specs, check_vma=False)
```
